32 devices in a mesh: wide: 8 (over z, y), lev: 4 (over x, core).
Axes of the slice: x: 2, y: 2, z: 4, core: 2. Of those that a mesh axis runs over, the one named last changes fastest.
Arguments:
- ensemble: float32 [128, 64, 1024], P(None, 'lev', 'wide'), may hold values from -6 to 6
- innovation: float32 [64, 1024], P('lev', 'wide'), may hold values from -0.4 to 0.4
- obs_inverse: float32 [64, 1024], P('lev', 'wide'), may hold values from 100 to 600
- root_tiles: float32 [8, 128, 128], replicated, may hold values from -0.1875 to 0.1875
- col_index: int32 [8, 8], replicated, may hold values from 0 to 7
- vert_weight: float32 [9, 64], replicated, may hold values from -1 to 1
- member_weight: float32 [128], replicated, may hold values from 0.04 to 0.1
- obs_blocks: int32 [8], replicated, may hold values from 0 to 7
Outputs:
- control: float32 [128, 64, 1024], P(None, 'lev', 'wide')
- increment: float32 [64, 1024], P('lev', 'wide')
The draws below stay inside these ranges and needn't reach their ends.
Inputs may be any that keep to these rules, and one draw needn't show every extreme that they name: `col_index`: column block numbers; repeats allowed. `obs_blocks`: observed column block numbers; a block listed several times counts that many times.
All inputs are finite; a program needn't handle non-finite values.
Results may differ from the reference program's by a relative error of at most 0.0001.
Values sent between devices are 32-bit elements; how exact they have to be, the bound alone decides.
No kernel may reach another device: no remote copies, remote signals or barrier semaphores. Data moves between devices by JAX's collectives and lax.ppermute only.
A program may use at most 128 MiB of HBM per device.

```python
import math
import jax
import jax.numpy as jnp
from jax import lax

MEMBERS = 128
LEVELS = 64
COLUMNS = 1024
BLOCK = 128
SLOTS = 8
ROW_BLOCKS = 8
OBS = 8
STEPS = 1


def plant(drawn, stream_key, least, top_value):
    dims = drawn.shape
    place = [jax.random.randint(jax.random.fold_in(stream_key, axis), (), 0, dims[axis]) for axis in range(len(dims))]
    drawn = drawn.at[tuple(place)].set(least)
    longest = dims.index(max(dims))
    place[longest] = (place[longest] + 1) % dims[longest]
    return drawn.at[tuple(place)].set(top_value)


def steps_of(rng, shape, cuts, smallest, largest):
    loudness = 1.0
    for dim, blocks in cuts:
        heights = jax.random.uniform(jax.random.fold_in(jax.random.fold_in(rng, 6), dim), (blocks,), jnp.float32, smallest / len(cuts), largest / len(cuts))
        loudness = loudness * jnp.repeat(jnp.exp(heights), shape[dim] // blocks).reshape((-1,) + (1,) * (len(shape) - 1 - dim))
    return loudness


def gaussian(own_key, shape, deviation, reach, cuts=(), kind=jnp.bfloat16):
    entries = jax.random.normal(own_key, shape, jnp.float32) * deviation
    if len(cuts) > 0:
        entries = steps_of(own_key, shape, cuts, -0.22, 0.18) * entries
    return jnp.clip(entries, min=-reach, max=reach).astype(kind)


def setup_inputs(seed: int = 0) -> dict:
    splits = jax.random.split(jax.random.key(seed), 9)
    return {
        "ensemble": gaussian(splits[0], (MEMBERS, LEVELS, COLUMNS), 1.0, 6.0, ((1, 4), (2, 8)), jnp.float32),
        "innovation": gaussian(splits[1], (LEVELS, COLUMNS), 0.05, 0.4, ((0, 4), (1, 8)), jnp.float32),
        "obs_inverse": jnp.clip(jnp.exp(math.log(600.0) - 1.7917595 * jax.random.uniform(splits[2], (LEVELS, COLUMNS), jnp.float32) ** steps_of(splits[2], (LEVELS, COLUMNS), ((0, 4), (1, 8)), -0.2, 0.2)), 100.0, 600.0),
        "root_tiles": gaussian(splits[3], (SLOTS, BLOCK, BLOCK), (BLOCK * SLOTS) ** -0.5, 0.1875, (), jnp.float32),
        "col_index": plant(jax.random.randint(splits[4], (ROW_BLOCKS, SLOTS), 0, ROW_BLOCKS), jax.random.fold_in(splits[4], 1), 0, ROW_BLOCKS - 1).astype(jnp.int32),
        "vert_weight": gaussian(splits[5], (9, LEVELS), 0.333, 1.0, (), jnp.float32),
        "member_weight": jnp.clip(jnp.exp(jax.random.uniform(splits[6], (MEMBERS,), jnp.float32, math.log(0.04), math.log(0.1))), 0.04, 0.1),
        "obs_blocks": plant(jax.random.randint(splits[7], (OBS,), 0, ROW_BLOCKS), jax.random.fold_in(splits[7], 1), 0, ROW_BLOCKS - 1).astype(jnp.int32),
    }


def horizontal(values, root_tiles, col_index):
    levels = values.shape[0]
    blocks = values.reshape(levels, -1, BLOCK)
    summed = jnp.zeros(blocks.shape, jnp.float32)
    for neighbor in range(SLOTS):
        picked = jnp.take(blocks, col_index[:, neighbor], axis=1)
        product = jnp.dot(picked.reshape(-1, BLOCK), root_tiles[neighbor], precision=lax.Precision.HIGHEST, preferred_element_type=jnp.float32)
        summed = summed + product.reshape(blocks.shape)
    return summed.reshape(values.shape)


def horizontal_t(values, root_tiles, col_index):
    levels = values.shape[0]
    blocks = values.reshape(levels, -1, BLOCK)
    flat = blocks.reshape(-1, BLOCK)
    summed = jnp.zeros(blocks.shape, jnp.float32)
    for neighbor in range(SLOTS):
        product = jnp.dot(flat, root_tiles[neighbor].T, precision=lax.Precision.HIGHEST, preferred_element_type=jnp.float32)
        summed = summed.at[:, col_index[:, neighbor], :].add(product.reshape(blocks.shape))
    return summed.reshape(values.shape)


def vertical(values, vert_weight):
    padded = jnp.pad(values, ((4, 4), (0, 0)))
    summed = jnp.zeros(values.shape, jnp.float32)
    for offset in range(9):
        summed = summed + vert_weight[offset][:, None] * padded[offset:offset + LEVELS]
    return summed


def vertical_t(values, vert_weight):
    summed = jnp.zeros(values.shape, jnp.float32)
    for offset in range(9):
        padded = jnp.pad(vert_weight[offset][:, None] * values, ((4, 4), (0, 0)))
        summed = summed + padded[8 - offset:8 - offset + LEVELS]
    return summed


def reference(ensemble, innovation, obs_inverse, root_tiles, col_index, vert_weight, member_weight, obs_blocks):
    block_ids = jnp.arange(ROW_BLOCKS, dtype=jnp.int32)
    counts = jnp.sum((obs_blocks[:, None] == block_ids[None, :]).astype(jnp.float32), axis=0)
    obs_weight = obs_inverse * jnp.repeat(counts, BLOCK)[None, :]
    weighted = member_weight[:, None, None] * ensemble

    def forward(control_field):
        def accumulate(carry, pieces):
            member_control, member_ens = pieces
            mapped = horizontal(vertical(member_control, vert_weight), root_tiles, col_index)
            return carry + member_ens * mapped, None

        summed, unused = lax.scan(accumulate, jnp.zeros((LEVELS, COLUMNS), jnp.float32), (control_field, weighted))
        return summed

    def adjoint(field_values):
        def one_member(member_ens):
            return vertical_t(horizontal_t(member_ens * field_values, root_tiles, col_index), vert_weight)

        return lax.map(one_member, weighted)

    gradient = adjoint(-(obs_weight * innovation))
    control = jnp.zeros((MEMBERS, LEVELS, COLUMNS), jnp.float32)
    increment = jnp.zeros((LEVELS, COLUMNS), jnp.float32)
    for iteration in range(STEPS):
        image_field = forward(gradient)
        gradient_image = gradient + adjoint(obs_weight * image_field)
        step_size = jnp.sum(gradient * gradient) / jnp.sum(gradient * gradient_image)
        control = control - step_size * gradient
        increment = increment - step_size * image_field
        gradient = gradient - step_size * gradient_image
    return control, increment
```

```python
import functools

import jax
import jax.numpy as jnp
from jax import lax
from jax.experimental import pallas as pl
from jax.experimental.pallas import tpu as pltpu
from jax.sharding import PartitionSpec as P

TAPS = 9
REACH = 4
CHUNKS = 1
DENSE_LIMIT = 2048


def with_halo(block, sides, width):
    for axis, dim in sides:
        count = lax.axis_size(axis)
        forward = [(i, i + 1) for i in range(count - 1)]
        backward = [(target, source) for source, target in forward]
        low = lax.ppermute(
            lax.slice_in_dim(block, block.shape[dim] - width, None, axis=dim), axis, forward
        )
        high = lax.ppermute(lax.slice_in_dim(block, 0, width, axis=dim), axis, backward)
        block = jnp.concatenate([low, block, high], axis=dim)
    return block


def horizontal(values, root_tiles, col_index):
    slot_count, block_size = (root_tiles.shape[0], root_tiles.shape[1])
    members, levels, columns = values.shape
    row_blocks = columns // block_size
    blocks = values.reshape(members, levels, row_blocks, block_size)
    picked = jnp.take(blocks, col_index.reshape(-1), axis=2)
    picked = picked.reshape(members * levels * row_blocks, slot_count * block_size)
    stacked = root_tiles.reshape(slot_count * block_size, block_size)
    product = jnp.dot(
        picked, stacked, precision=lax.Precision.HIGHEST, preferred_element_type=jnp.float32
    )
    return product.reshape(values.shape)


def horizontal_t(values, root_tiles, col_index):
    slot_count, block_size = (root_tiles.shape[0], root_tiles.shape[1])
    members, levels, columns = values.shape
    row_blocks = columns // block_size
    flat = values.reshape(-1, block_size)
    stacked = jnp.transpose(root_tiles, (2, 0, 1)).reshape(block_size, slot_count * block_size)
    product = jnp.dot(
        flat, stacked, precision=lax.Precision.HIGHEST, preferred_element_type=jnp.float32
    )
    product = product.reshape(members, levels, row_blocks * slot_count, block_size)
    summed = jnp.zeros((members, levels, row_blocks, block_size), jnp.float32)
    summed = summed.at[:, :, col_index.reshape(-1), :].add(product)
    return summed.reshape(values.shape)


def general_body(
    ensemble, innovation, obs_inverse, root_tiles, col_index, vert_weight, member_weight, obs_blocks
):
    block_size = root_tiles.shape[1]
    lev_dev = ensemble.shape[1]
    col_dev = ensemble.shape[2]
    wide_count = lax.axis_size("wide")
    first_block = lax.axis_index("wide") * (col_dev // block_size)
    block_ids = first_block + jnp.arange(col_dev // block_size, dtype=jnp.int32)
    counts = jnp.sum((obs_blocks[:, None] == block_ids[None, :]).astype(jnp.float32), axis=0)
    obs_weight = obs_inverse * jnp.repeat(counts, block_size)[None, :]
    padded_weights = jnp.pad(vert_weight, ((0, 0), (4, 4)))
    level_start = lax.axis_index("lev") * lev_dev
    wide_weights = lax.dynamic_slice_in_dim(padded_weights, level_start, lev_dev + 8, 1)
    own_weights = wide_weights[:, 4 : 4 + lev_dev]
    weighted = member_weight[:, None, None] * ensemble

    def grouped(values):
        return values.reshape(wide_count, values.shape[0] // wide_count, lev_dev, col_dev)

    values = lax.all_to_all(
        grouped(weighted * (-(obs_weight * innovation))[None]),
        "wide",
        split_axis=0,
        concat_axis=3,
        tiled=True,
    )[0]
    blended = horizontal_t(values, root_tiles, col_index)
    padded = with_halo(blended, (("lev", 1),), 4)
    summed = jnp.zeros(values.shape, jnp.float32)
    for reverse_offset in range(9):
        lower = 8 - reverse_offset
        summed = (
            summed
            + wide_weights[reverse_offset, lower : lower + lev_dev][None, :, None]
            * padded[:, lower : lower + lev_dev]
        )
    member_fields = summed[None]
    gradient = lax.all_to_all(member_fields[0], "wide", split_axis=2, concat_axis=0, tiled=True)
    control = jnp.zeros_like(gradient)
    increment = jnp.zeros_like(innovation)
    values = lax.all_to_all(grouped(gradient), "wide", split_axis=0, concat_axis=3, tiled=True)[0]
    padded = with_halo(values, (("lev", 1),), 4)
    blended = jnp.zeros(values.shape, jnp.float32)
    for offset in range(9):
        blended = (
            blended + own_weights[offset][None, :, None] * padded[:, offset : offset + lev_dev]
        )
    mapped = horizontal(blended, root_tiles, col_index)[None]
    by_column = lax.all_to_all(mapped[0], "wide", split_axis=2, concat_axis=0, tiled=True)
    image_field = jnp.sum(weighted * by_column, axis=0)
    grad_norm, observed = lax.psum(
        (jnp.sum(gradient * gradient), jnp.sum(obs_weight * image_field * image_field)),
        ("wide", "lev"),
    )
    curvature = grad_norm + observed
    step_size = grad_norm / curvature
    control = control - step_size * gradient
    increment = increment - step_size * image_field
    return (control, increment)


def split_high_low(values):
    high = values.astype(jnp.bfloat16)
    return high, (values - high.astype(jnp.float32)).astype(jnp.bfloat16)


def root_kernel(col_ref, tiles_ref, high_ref, low_ref, root):
    blocks, slots = col_ref.shape
    size = tiles_ref.shape[1]
    root[...] = jnp.zeros_like(root)

    @pl.loop(0, slots)
    def _(slot):
        tile = tiles_ref[slot]
        for row in range(blocks):
            root[col_ref[row, slot], :, row * size : (row + 1) * size] += tile

    @pl.loop(0, blocks)
    def _(block):
        high, low = split_high_low(root[block])
        start = pl.multiple_of(block * size, size)
        high_ref[pl.ds(start, size), :] = high
        low_ref[pl.ds(start, size), :] = low


def dense_root(root_tiles, col_index):
    size = root_tiles.shape[1]
    blocks = col_index.shape[0]
    columns = blocks * size
    part = jax.ShapeDtypeStruct((columns, columns), jnp.bfloat16)
    return pl.pallas_call(
        root_kernel,
        out_shape=(part, part),
        in_specs=[
            pl.BlockSpec(memory_space=pltpu.SMEM),
            pl.BlockSpec(memory_space=pltpu.VMEM),
        ],
        out_specs=[pl.BlockSpec(memory_space=pltpu.VMEM)] * 2,
        scratch_shapes=[pltpu.VMEM((blocks, size, columns), jnp.float32)],
        cost_estimate=pl.CostEstimate(
            flops=8 * columns * columns, bytes_accessed=8 * columns * columns, transcendentals=0
        ),
    )(col_index, root_tiles)


def vertical_taps(vert_weight):
    levels = vert_weight.shape[1]
    level = jnp.arange(levels)
    padded = jnp.pad(vert_weight, ((0, 0), (REACH, REACH)))
    forward, backward = [], []
    for tap in range(TAPS):
        shift = tap - REACH
        inside = (level + shift >= 0) & (level + shift < levels)
        forward.append(jnp.where(inside, vert_weight[tap], 0.0))
        backward.append(padded[TAPS - 1 - tap, tap : tap + levels])
    return jnp.stack(forward + backward, axis=1)


def vertical(values, taps, first):
    levels = values.shape[0]
    total = taps[first + REACH] * values
    for tap in range(TAPS):
        shift = tap - REACH
        if shift != 0:
            total = total + taps[first + tap] * pltpu.roll(values, (-shift) % levels, 0)
    return total


def three_pass(parts, rows, high, low, contract):
    dims = (((1,), (contract,)), ((), ()))
    both = lax.dot_general(parts[...], high, dims, preferred_element_type=jnp.float32)
    small = lax.dot_general(parts[:rows, :], low, dims, preferred_element_type=jnp.float32)
    return both[:rows] + (both[rows:] + small)


def member_kernel(
    weight_ref,
    ens_ref,
    innov_ref,
    taps_ref,
    high_any,
    low_any,
    sofar_ref,
    grad_ref,
    image_ref,
    norm_ref,
    high,
    low,
    taps,
    parts,
    field,
    sems,
):
    devices, members, lev_dev, size = grad_ref.shape
    columns = high.shape[0]
    wide = columns // size
    lev_count = devices // wide
    levels = lev_dev * lev_count
    rows = members * levels
    step = min(2 * size, columns)
    copies = [
        pltpu.make_async_copy(high_any, high, sems.at[0]),
        pltpu.make_async_copy(low_any, low, sems.at[1]),
    ]
    for copy in copies:
        copy.start()
    for tap in range(2 * TAPS):
        taps[tap] = jnp.broadcast_to(taps_ref[:, tap : tap + 1], (levels, size))

    def store_parts(member, lanes, values):
        first, second = split_high_low(values)
        parts[member * levels : (member + 1) * levels, lanes] = first
        parts[rows + member * levels : rows + (member + 1) * levels, lanes] = second

    @pl.loop(0, wide)
    def _(block):
        lanes = pl.ds(pl.multiple_of(block * size, size), size)
        for member in range(members):
            pieces = [
                ens_ref[block * lev_count + lev, member] * innov_ref[block * lev_count + lev, 0]
                for lev in range(lev_count)
            ]
            product = weight_ref[member] * jnp.concatenate(pieces, axis=0)
            store_parts(member, lanes, vertical(product, taps, TAPS))

    for copy in copies:
        copy.wait()
    for start in range(0, columns, step):
        field[:, start : start + step] = three_pass(
            parts, rows, high[start : start + step, :], low[start : start + step, :], 1
        )
    norm_ref[...] = jnp.zeros_like(norm_ref)

    @pl.loop(0, wide)
    def _(block):
        lanes = pl.ds(pl.multiple_of(block * size, size), size)
        for member in range(members):
            values = field[member * levels : (member + 1) * levels, lanes]
            for lev in range(lev_count):
                grad_ref[block * lev_count + lev, member] = values[
                    lev * lev_dev : (lev + 1) * lev_dev
                ]
            squares = values * values
            norm_ref[...] += jnp.sum(squares.reshape(-1, 8, size), axis=0)
            store_parts(member, lanes, vertical(values, taps, 0))

    for start in range(0, columns, step):
        field[:, start : start + step] = three_pass(
            parts, rows, high[:, start : start + step], low[:, start : start + step], 0
        )

    @pl.loop(0, wide)
    def _(block):
        lanes = pl.ds(pl.multiple_of(block * size, size), size)
        for lev in range(lev_count):
            total = sofar_ref[block * lev_count + lev]
            for member in range(members):
                start = member * levels + lev * lev_dev
                total = total + (
                    weight_ref[member] * ens_ref[block * lev_count + lev, member]
                ) * field[start : start + lev_dev, lanes]
            image_ref[block * lev_count + lev] = total


def whole_spec(shape, index=None):
    index = index or (0,) * len(shape)
    return pl.BlockSpec(shape, lambda i: index)


def member_part(weights, ens, innov_source, slot, taps, high, low, sofar, members):
    devices, _, lev_dev, size = ens.shape
    columns = high.shape[0]
    levels = taps.shape[0]
    rows = members * levels
    grad = jax.ShapeDtypeStruct((devices, members, lev_dev, size), jnp.float32)
    image = jax.ShapeDtypeStruct((devices, lev_dev, size), jnp.float32)
    norm = jax.ShapeDtypeStruct((8, size), jnp.float32)
    return pl.pallas_call(
        member_kernel,
        grid=(1,),
        out_shape=(grad, image, norm),
        in_specs=[
            pl.BlockSpec(memory_space=pltpu.SMEM),
            whole_spec((devices, members, lev_dev, size)),
            whole_spec((devices, 1, lev_dev, size), (0, slot, 0, 0)),
            whole_spec(taps.shape),
            pl.BlockSpec(memory_space=pl.ANY),
            pl.BlockSpec(memory_space=pl.ANY),
            whole_spec(image.shape),
        ],
        out_specs=[whole_spec(grad.shape), whole_spec(image.shape), whole_spec(norm.shape)],
        scratch_shapes=[
            pltpu.VMEM((columns, columns), jnp.bfloat16),
            pltpu.VMEM((columns, columns), jnp.bfloat16),
            pltpu.VMEM((2 * TAPS, levels, size), jnp.float32),
            pltpu.VMEM((2 * rows, columns), jnp.bfloat16),
            pltpu.VMEM((rows, columns), jnp.float32),
            pltpu.SemaphoreType.DMA((2,)),
        ],
        cost_estimate=pl.CostEstimate(
            flops=12 * rows * columns * columns,
            bytes_accessed=4 * columns * columns + 8 * rows * columns,
            transcendentals=0,
        ),
    )(weights, ens, innov_source, taps, high, low, sofar)


def member_body(
    ensemble, innovation, obs_inverse, root_tiles, col_index, vert_weight, member_weight, obs_blocks
):
    axes = ("wide", "lev")
    devices = lax.axis_size(axes)
    members, lev_dev, size = ensemble.shape
    per_device = members // devices
    chunks = CHUNKS if per_device % CHUNKS == 0 else 1
    part = per_device // chunks
    counts = jnp.sum((obs_blocks == lax.axis_index("wide")).astype(jnp.float32))
    obs_weight = obs_inverse * counts
    source = -(obs_weight * innovation)
    grouped = ensemble.reshape(devices, per_device, lev_dev, size)
    exchange = functools.partial(
        lax.all_to_all, axis_name=axes, split_axis=0, concat_axis=0, tiled=True
    )
    first = jnp.concatenate(
        [grouped[:, :part], jnp.broadcast_to(source, (devices, 1, lev_dev, size))], axis=1
    )
    arrived = [exchange(first)]
    for chunk in range(1, chunks):
        arrived.append(exchange(grouped[:, chunk * part : (chunk + 1) * part]))
    high, low = dense_root(root_tiles, col_index)
    taps = vertical_taps(vert_weight)
    own_weights = lax.dynamic_slice_in_dim(
        member_weight, lax.axis_index(axes) * per_device, per_device
    )
    image = jnp.zeros((devices, lev_dev, size), jnp.float32)
    grads, norms = [], []
    for chunk in range(chunks):
        grad, image, norm = member_part(
            own_weights[chunk * part : (chunk + 1) * part],
            arrived[chunk],
            arrived[0],
            part,
            taps,
            high,
            low,
            image,
            part,
        )
        grads.append(grad)
        norms.append(norm)
    image = jnp.sum(exchange(image), axis=0)
    returned = [exchange(grad) for grad in grads]
    grad_norm = sum(jnp.sum(norm) for norm in norms)
    observed = jnp.sum(obs_weight * image * image)
    lane = jnp.arange(size)
    scalars = jnp.where(lane == 0, grad_norm, jnp.where(lane == 1, observed, 0.0))
    totals = jnp.sum(exchange(jnp.broadcast_to(scalars, (devices, size))), axis=0)
    step_size = totals[0] / (totals[0] + totals[1])
    control = -step_size * jnp.concatenate(returned, axis=1).reshape(ensemble.shape)
    increment = -step_size * image
    return (control, increment)


def solution(mesh):
    in_specs = (P(None, "lev", "wide"), P("lev", "wide"), P("lev", "wide"), P(), P(), P(), P(), P())
    out_specs = (P(None, "lev", "wide"), P("lev", "wide"))

    def body(*args):
        ensemble, root_tiles = args[0], args[3]
        devices = lax.axis_size(("wide", "lev"))
        columns = ensemble.shape[2] * lax.axis_size("wide")
        fits = (
            ensemble.shape[0] % devices == 0
            and ensemble.shape[2] == root_tiles.shape[1]
            and root_tiles.shape[1] == 128
            and ensemble.shape[1] % 8 == 0
            and columns <= DENSE_LIMIT
        )
        return member_body(*args) if fits else general_body(*args)

    return jax.shard_map(body, mesh=mesh, in_specs=in_specs, out_specs=out_specs, check_vma=False)
```

```python
import functools

import jax
import jax.numpy as jnp
from jax import lax
from jax.experimental import pallas as pl
from jax.experimental.pallas import tpu as pltpu
from jax.sharding import PartitionSpec as P

TAPS = 9
REACH = 4
ARRIVE = (3, 2, 1, 7, 6, 5, 4)
SPANS = ((0, 4), (4, 8))


def with_halo(block, sides, width):
    for axis, dim in sides:
        count = lax.axis_size(axis)
        forward = [(i, i + 1) for i in range(count - 1)]
        backward = [(target, source) for source, target in forward]
        low = lax.ppermute(
            lax.slice_in_dim(block, block.shape[dim] - width, None, axis=dim), axis, forward
        )
        high = lax.ppermute(lax.slice_in_dim(block, 0, width, axis=dim), axis, backward)
        block = jnp.concatenate([low, block, high], axis=dim)
    return block


def horizontal(values, root_tiles, col_index):
    slot_count, block_size = (root_tiles.shape[0], root_tiles.shape[1])
    members, levels, columns = values.shape
    row_blocks = columns // block_size
    blocks = values.reshape(members, levels, row_blocks, block_size)
    picked = jnp.take(blocks, col_index.reshape(-1), axis=2)
    picked = picked.reshape(members * levels * row_blocks, slot_count * block_size)
    stacked = root_tiles.reshape(slot_count * block_size, block_size)
    product = jnp.dot(
        picked, stacked, precision=lax.Precision.HIGHEST, preferred_element_type=jnp.float32
    )
    return product.reshape(values.shape)


def horizontal_t(values, root_tiles, col_index):
    slot_count, block_size = (root_tiles.shape[0], root_tiles.shape[1])
    members, levels, columns = values.shape
    row_blocks = columns // block_size
    flat = values.reshape(-1, block_size)
    stacked = jnp.transpose(root_tiles, (2, 0, 1)).reshape(block_size, slot_count * block_size)
    product = jnp.dot(
        flat, stacked, precision=lax.Precision.HIGHEST, preferred_element_type=jnp.float32
    )
    product = product.reshape(members, levels, row_blocks * slot_count, block_size)
    summed = jnp.zeros((members, levels, row_blocks, block_size), jnp.float32)
    summed = summed.at[:, :, col_index.reshape(-1), :].add(product)
    return summed.reshape(values.shape)


def general_body(
    ensemble, innovation, obs_inverse, root_tiles, col_index, vert_weight, member_weight, obs_blocks
):
    block_size = root_tiles.shape[1]
    lev_dev = ensemble.shape[1]
    col_dev = ensemble.shape[2]
    wide_count = lax.axis_size("wide")
    first_block = lax.axis_index("wide") * (col_dev // block_size)
    block_ids = first_block + jnp.arange(col_dev // block_size, dtype=jnp.int32)
    counts = jnp.sum((obs_blocks[:, None] == block_ids[None, :]).astype(jnp.float32), axis=0)
    obs_weight = obs_inverse * jnp.repeat(counts, block_size)[None, :]
    padded_weights = jnp.pad(vert_weight, ((0, 0), (4, 4)))
    level_start = lax.axis_index("lev") * lev_dev
    wide_weights = lax.dynamic_slice_in_dim(padded_weights, level_start, lev_dev + 8, 1)
    own_weights = wide_weights[:, 4 : 4 + lev_dev]
    weighted = member_weight[:, None, None] * ensemble

    def grouped(values):
        return values.reshape(wide_count, values.shape[0] // wide_count, lev_dev, col_dev)

    values = lax.all_to_all(
        grouped(weighted * (-(obs_weight * innovation))[None]),
        "wide",
        split_axis=0,
        concat_axis=3,
        tiled=True,
    )[0]
    blended = horizontal_t(values, root_tiles, col_index)
    padded = with_halo(blended, (("lev", 1),), 4)
    summed = jnp.zeros(values.shape, jnp.float32)
    for reverse_offset in range(9):
        lower = 8 - reverse_offset
        summed = (
            summed
            + wide_weights[reverse_offset, lower : lower + lev_dev][None, :, None]
            * padded[:, lower : lower + lev_dev]
        )
    member_fields = summed[None]
    gradient = lax.all_to_all(member_fields[0], "wide", split_axis=2, concat_axis=0, tiled=True)
    control = jnp.zeros_like(gradient)
    increment = jnp.zeros_like(innovation)
    values = lax.all_to_all(grouped(gradient), "wide", split_axis=0, concat_axis=3, tiled=True)[0]
    padded = with_halo(values, (("lev", 1),), 4)
    blended = jnp.zeros(values.shape, jnp.float32)
    for offset in range(9):
        blended = (
            blended + own_weights[offset][None, :, None] * padded[:, offset : offset + lev_dev]
        )
    mapped = horizontal(blended, root_tiles, col_index)[None]
    by_column = lax.all_to_all(mapped[0], "wide", split_axis=2, concat_axis=0, tiled=True)
    image_field = jnp.sum(weighted * by_column, axis=0)
    grad_norm, observed = lax.psum(
        (jnp.sum(gradient * gradient), jnp.sum(obs_weight * image_field * image_field)),
        ("wide", "lev"),
    )
    curvature = grad_norm + observed
    step_size = grad_norm / curvature
    control = control - step_size * gradient
    increment = increment - step_size * image_field
    return (control, increment)


SPREAD_ROOM = 8
PREPARE_ROOM = 16
MEMBER_ROOM = 24
FINISH_ROOM = 8


def split_high_low(values):
    high = values.astype(jnp.bfloat16)
    return high, (values - high.astype(jnp.float32)).astype(jnp.bfloat16)


SCALARS = pl.BlockSpec(memory_space=pltpu.SMEM)
IN_PLACE = pl.BlockSpec(memory_space=pltpu.HBM)
ON_CHIP = pl.BlockSpec(memory_space=pltpu.VMEM)


def in_place(operand):
    return pltpu.with_memory_space_constraint(operand, pltpu.HBM)


def room(mebibytes):
    return pltpu.CompilerParams(vmem_limit_bytes=mebibytes << 20)


def spread_kernel(ens_any, inverse_any, innov_any, seen_any, *refs):
    wide = ens_any.shape[0]
    blocks, weight_ref, (innov, seen, sems) = refs[:wide], refs[wide], refs[wide + 1 :]
    members = ens_any.shape[1]
    place = lax.axis_index("wide")
    small = [
        pltpu.make_async_copy(seen_any, seen, sems.at[wide]),
        pltpu.make_async_copy(inverse_any, weight_ref, sems.at[wide + 1]),
        pltpu.make_async_copy(innov_any, innov, sems.at[wide + 2]),
    ]
    fetches = [
        pltpu.make_async_copy(
            ens_any.at[place ^ other], blocks[other].at[pl.ds(0, members)], sems.at[other]
        )
        for other in (*ARRIVE, 0)
        if other < wide
    ]
    for fetch in small + fetches:
        fetch.start()
    for fetch in small:
        fetch.wait()
    count = lax.fori_loop(
        0,
        seen.shape[0],
        lambda i, total: total + (seen[i] == place).astype(jnp.int32),
        jnp.int32(0),
    )
    weight = weight_ref[...] * count.astype(jnp.float32)
    weight_ref[...] = weight
    source = -(weight * innov[...])
    for block in blocks:
        block[members] = source
    for fetch in fetches:
        fetch.wait()


def spread(ensemble, obs_inverse, innovation, obs_blocks):
    wide, members, lev_dev, size = ensemble.shape
    block = jax.ShapeDtypeStruct((members + 1, lev_dev, size), jnp.float32)
    own = jax.ShapeDtypeStruct((lev_dev, size), jnp.float32)
    return pl.pallas_call(
        spread_kernel,
        out_shape=[block] * wide + [own],
        in_specs=[IN_PLACE] * 4,
        out_specs=[ON_CHIP] * (wide + 1),
        scratch_shapes=[
            pltpu.VMEM(own.shape, jnp.float32),
            pltpu.SMEM(obs_blocks.shape, jnp.int32),
            pltpu.SemaphoreType.DMA((wide + 3,)),
        ],
        compiler_params=room(SPREAD_ROOM),
        cost_estimate=pl.CostEstimate(
            flops=0, bytes_accessed=8 * ensemble.size, transcendentals=0
        ),
    )(*map(in_place, (ensemble, obs_inverse, innovation, obs_blocks)))


def prepare_kernel(
    col_any, tiles_any, weight_ref, high_ref, low_ref, taps_ref, root, col_ref, tiles_ref, sems
):
    blocks, slots = col_ref.shape
    size = tiles_ref.shape[1]
    fetches = [
        pltpu.make_async_copy(col_any, col_ref, sems.at[0]),
        pltpu.make_async_copy(tiles_any, tiles_ref, sems.at[1]),
    ]
    for fetch in fetches:
        fetch.start()
    lev_dev = taps_ref.shape[1] - 2 * REACH
    place, level_start = lax.axis_index("wide"), lax.axis_index("lev") * lev_dev
    root[...] = jnp.zeros_like(root)
    for fetch in fetches:
        fetch.wait()

    @pl.loop(0, slots)
    def _(slot):
        tile = tiles_ref[slot]
        for row in range(blocks):
            lanes = pl.ds(pl.multiple_of((row ^ place) * size, size), size)
            root[col_ref[row, slot] ^ place, :, lanes] += tile

    @pl.loop(0, blocks)
    def _(block):
        high, low = split_high_low(root[block])
        start = pl.multiple_of(block * size, size)
        high_ref[pl.ds(start, size), :] = high
        low_ref[pl.ds(start, size), :] = low

    outer = taps_ref.shape[1]
    levels = weight_ref.shape[0] - 4 * REACH
    window = weight_ref[pl.ds(pl.multiple_of(level_start, 8), lev_dev + 4 * REACH), :]
    target = level_start - REACH + lax.broadcasted_iota(jnp.int32, (outer, size), 0)
    inside = (target >= 0) & (target < levels)
    own = window[2 * REACH :]
    for tap in range(TAPS):
        column = pltpu.roll(window, (-tap) % window.shape[0], 0)[:outer] if tap else window[:outer]
        column = column[:, TAPS - 1 - tap : TAPS - tap]
        taps_ref[tap] = jnp.where(inside, jnp.broadcast_to(column, (outer, size)), 0.0)
        taps_ref[TAPS + tap] = jnp.broadcast_to(own[:outer, tap : tap + 1], (outer, size))


def prepare(root_tiles, col_index, vert_weight, lev_dev):
    size = root_tiles.shape[1]
    blocks = col_index.shape[0]
    columns = blocks * size
    outer = lev_dev + 2 * REACH
    weights = jnp.pad(vert_weight.T, ((2 * REACH, 2 * REACH), (0, 128 - TAPS)))
    part = jax.ShapeDtypeStruct((columns, columns), jnp.bfloat16)
    taps = jax.ShapeDtypeStruct((2 * TAPS, outer, size), jnp.float32)
    return pl.pallas_call(
        prepare_kernel,
        out_shape=(part, part, taps),
        in_specs=[IN_PLACE, IN_PLACE, ON_CHIP],
        out_specs=[ON_CHIP] * 3,
        scratch_shapes=[
            pltpu.VMEM((blocks, size, columns), jnp.float32),
            pltpu.SMEM(col_index.shape, jnp.int32),
            pltpu.VMEM(root_tiles.shape, jnp.float32),
            pltpu.SemaphoreType.DMA((2,)),
        ],
        compiler_params=room(PREPARE_ROOM),
        cost_estimate=pl.CostEstimate(
            flops=8 * columns * columns, bytes_accessed=8 * columns * columns, transcendentals=0
        ),
    )(in_place(col_index), in_place(root_tiles), weights)


def vertical(values, taps, first, count):
    rows = values.shape[0]
    total = taps[first, :count] * values[:count]
    for tap in range(1, TAPS):
        total = total + taps[first + tap, :count] * pltpu.roll(values, rows - tap, 0)[:count]
    return total


def three_pass(parts, rows, high, low, contract):
    dims = (((1,), (contract,)), ((), ()))
    both = lax.dot_general(parts[...], high, dims, preferred_element_type=jnp.float32)
    small = lax.dot_general(parts[:rows, :], low, dims, preferred_element_type=jnp.float32)
    return both[:rows] + (both[rows:] + small)


def gradient_kernel(begin, first, weight_ref, taps_ref, high, low, below, above, *refs):
    count = below.shape[0]
    ens, refs = refs[:count], refs[count:]
    if not first:
        sofar, refs = refs[0], refs[1:]
    field, parts, grads = refs[0], refs[-1], refs[1:-1]
    slots, lev_dev, size = ens[0].shape
    members = slots - 1
    columns = high.shape[0]
    outer = lev_dev + 2 * REACH
    rows = members * outer
    first_weight = lax.axis_index("wide") * members
    for block in range(count):

        def extended(member):
            pieces = [below[block, member], ens[block][member], above[block, member]]
            return jnp.concatenate(pieces, axis=0)

        source = extended(members)
        lanes = slice(block * size, (block + 1) * size)

        @pl.loop(0, members // 2)
        def _(pair):
            pieces = []
            for half in range(2):
                member = 2 * pair + half
                product = weight_ref[first_weight + member] * (extended(member) * source)
                pieces.append(vertical(product, taps_ref, 0, outer))
            upper, lower = split_high_low(jnp.concatenate(pieces, axis=0))
            start = pl.multiple_of(pair * 2 * outer, 2 * outer)
            parts[pl.ds(start, 2 * outer), lanes] = upper
            start = pl.multiple_of(rows + pair * 2 * outer, 2 * outer)
            parts[pl.ds(start, 2 * outer), lanes] = lower

    span = slice(begin * size, (begin + count) * size)
    step = min(2 * size, columns)
    for at in range(0, columns, step):
        total = three_pass(parts, rows, high[at : at + step, span], low[at : at + step, span], 1)
        if not first:
            total = total + sofar[:, at : at + step]
        field[:, at : at + step] = total
    for block, grad in enumerate(grads):
        lanes = slice(block * size, (block + 1) * size)
        for member in range(members):
            start = member * outer + REACH
            grad[member] = field[start : start + lev_dev, lanes]


def gradient_part(weights, taps, high, low, halo_pair, arrived, begin, sofar, last):
    slots, lev_dev, size = arrived[0].shape
    members = slots - 1
    columns = high.shape[0]
    rows = members * (lev_dev + 2 * REACH)
    field = jax.ShapeDtypeStruct((rows, columns), jnp.float32)
    grads = [jax.ShapeDtypeStruct((members, lev_dev, size), jnp.float32)] * (columns // size)
    outs = [field] + (grads if last else [])
    operands = [taps, high, low, *halo_pair, *arrived] + ([] if sofar is None else [sofar])
    span = len(arrived) * size
    return pl.pallas_call(
        functools.partial(gradient_kernel, begin, sofar is None),
        out_shape=outs,
        in_specs=[SCALARS] + [ON_CHIP] * len(operands),
        out_specs=[ON_CHIP] * len(outs),
        scratch_shapes=[pltpu.VMEM((2 * rows, span), jnp.bfloat16)],
        compiler_params=room(MEMBER_ROOM),
        cost_estimate=pl.CostEstimate(
            flops=6 * rows * columns * span, bytes_accessed=4 * rows * columns, transcendentals=0
        ),
    )(weights, *operands)


def image_kernel(weight_ref, taps_ref, high, low, field, *refs):
    ens, (image_ref, norm_ref, parts, mapped) = refs[:-4], refs[-4:]
    slots, lev_dev, size = ens[0].shape
    members = slots - 1
    columns = high.shape[0]
    outer = lev_dev + 2 * REACH
    first_weight = lax.axis_index("wide") * members
    rows = members * lev_dev
    norm_ref[...] = jnp.zeros_like(norm_ref)
    for block in range(len(ens)):
        lanes = slice(block * size, (block + 1) * size)

        @pl.loop(0, members)
        def _(member):
            values = field[pl.ds(pl.multiple_of(member * outer, 8), outer), lanes]
            own = pltpu.roll(values, outer - REACH, 0)[:lev_dev]
            norm_ref[...] += jnp.sum((own * own).reshape(-1, 8, size), axis=0)
            upper, lower = split_high_low(vertical(values, taps_ref, TAPS, lev_dev))
            parts[pl.ds(pl.multiple_of(member * lev_dev, lev_dev), lev_dev), lanes] = upper
            start = pl.multiple_of(rows + member * lev_dev, lev_dev)
            parts[pl.ds(start, lev_dev), lanes] = lower

    step = min(2 * size, columns)
    for at in range(0, columns, step):
        mapped[:, at : at + step] = three_pass(
            parts, rows, high[:, at : at + step], low[:, at : at + step], 0
        )
    for block in range(len(ens)):
        lanes = slice(block * size, (block + 1) * size)

        def add(member, total):
            start = pl.multiple_of(member * lev_dev, lev_dev)
            weighted = weight_ref[first_weight + member] * ens[block][member]
            return total + weighted * mapped[pl.ds(start, lev_dev), lanes]

        image_ref[block] = lax.fori_loop(
            0, members, add, jnp.zeros((lev_dev, size), jnp.float32), unroll=4
        )


def image_part(weights, taps, high, low, field, arrived):
    slots, lev_dev, size = arrived[0].shape
    columns = high.shape[0]
    rows = (slots - 1) * lev_dev
    return pl.pallas_call(
        image_kernel,
        out_shape=[
            jax.ShapeDtypeStruct((len(arrived), lev_dev, size), jnp.float32),
            jax.ShapeDtypeStruct((8, size), jnp.float32),
        ],
        in_specs=[SCALARS] + [ON_CHIP] * (4 + len(arrived)),
        out_specs=[ON_CHIP] * 2,
        scratch_shapes=[
            pltpu.VMEM((2 * rows, columns), jnp.bfloat16),
            pltpu.VMEM((rows, columns), jnp.float32),
        ],
        compiler_params=room(MEMBER_ROOM),
        cost_estimate=pl.CostEstimate(
            flops=6 * rows * columns * columns, bytes_accessed=4 * rows * columns, transcendentals=0
        ),
    )(weights, taps, high, low, field, *arrived)


def finish_kernel(image_ref, *refs):
    wide = (len(refs) - 4) // 2
    sums_refs, grad_refs, refs = refs[:wide], refs[wide : 2 * wide], refs[2 * wide :]
    control_any, increment_ref, scaled, sems = refs
    place = lax.axis_index("wide")
    sums = sum(sums_ref[...] for sums_ref in sums_refs)
    half = sums.shape[0] // 2
    norm = jnp.sum(sums[:half], keepdims=True)
    observed = jnp.sum(sums[half:], keepdims=True)
    scale = -(norm / (norm + observed))
    increment_ref[...] = scale * image_ref[...]
    stores = []
    for other, grad in enumerate(grad_refs):
        scaled[other] = scale[None] * grad[...]
        stores.append(
            pltpu.make_async_copy(scaled.at[other], control_any.at[place ^ other], sems.at[other])
        )
        stores[-1].start()
    for store in stores:
        store.wait()


def finish(image, sums, grads):
    wide = len(grads)
    control = jax.ShapeDtypeStruct((wide, *grads[0].shape), jnp.float32)
    return pl.pallas_call(
        finish_kernel,
        out_shape=(control, jax.ShapeDtypeStruct(image.shape, jnp.float32)),
        in_specs=[ON_CHIP] * (1 + 2 * wide),
        out_specs=[IN_PLACE, ON_CHIP],
        scratch_shapes=[
            pltpu.VMEM(control.shape, jnp.float32),
            pltpu.SemaphoreType.DMA((wide,)),
        ],
        compiler_params=room(FINISH_ROOM),
    )(image, *sums, *grads)


def swap(values, axes, other):
    count = lax.axis_size(axes)
    return lax.ppermute(values, axes, [(i, i ^ other) for i in range(count)])


def halos(arrived):
    reach = 2 * REACH
    count = lax.axis_size("lev")
    up = [(i, i + 1) for i in range(count - 1)]
    down = [(i + 1, i) for i in range(count - 1)]
    tops = jnp.stack([block[:, -reach:] for block in arrived])
    bottoms = jnp.stack([block[:, :reach] for block in arrived])
    below = lax.ppermute(tops, "lev", up)
    above = lax.ppermute(bottoms, "lev", down)
    return [below, above]


def member_body(
    ensemble, innovation, obs_inverse, root_tiles, col_index, vert_weight, member_weight, obs_blocks
):
    wide = lax.axis_size("wide")
    members, lev_dev, size = ensemble.shape
    part = members // wide
    *sent, obs_weight = spread(
        ensemble.reshape(wide, part, lev_dev, size), obs_inverse, innovation, obs_blocks
    )
    arrived = [sent[0]] + [None] * (wide - 1)
    for other in ARRIVE:
        if other < wide:
            arrived[other] = swap(sent[other], "wide", other)
    high, low, taps = prepare(root_tiles, col_index, vert_weight, lev_dev)
    results = (None,)
    for number, (begin, end) in enumerate(SPANS):
        group = arrived[begin * wide // 8 : end * wide // 8]
        halo_pair = halos(group)
        results = gradient_part(
            member_weight, taps, high, low, halo_pair, group, begin * wide // 8,
            results[0], number == len(SPANS) - 1,
        )
    field, *grads = results
    for other in range(1, wide):
        grads[other] = swap(grads[other], "wide", other)
    image, norm = image_part(member_weight, taps, high, low, field, arrived)
    other = wide // 2
    while other:
        image = image[:other] + swap(image[other:], "wide", other)
        other = other // 2
    image = image[0]
    observed = obs_weight * image * image
    sums = jnp.concatenate([norm, jnp.sum(observed.reshape(-1, 8, size), axis=0)], axis=0)
    other = 1
    while other < lax.axis_size("lev"):
        sums = sums + swap(sums, "lev", other)
        other = other * 2
    shares = [sums] + [swap(sums, "wide", other) for other in range(1, wide)]
    control, increment = finish(image, shares, grads)
    return control.reshape(ensemble.shape), increment


def solution(mesh):
    in_specs = (P(None, "lev", "wide"), P("lev", "wide"), P("lev", "wide"), P(), P(), P(), P(), P())
    out_specs = (P(None, "lev", "wide"), P("lev", "wide"))

    def body(*args):
        ensemble, root_tiles = args[0], args[3]
        wide, lev = lax.axis_size("wide"), lax.axis_size("lev")
        members, lev_dev, col_dev = ensemble.shape
        fits = (
            wide & (wide - 1) == 0
            and lev & (lev - 1) == 0
            and wide == 8
            and members % (2 * wide) == 0
            and lev_dev % 16 == 0
            and col_dev == root_tiles.shape[1] == 128
        )
        if not fits:
            return general_body(*args)
        return member_body(*args)

    return jax.shard_map(body, mesh=mesh, in_specs=in_specs, out_specs=out_specs, check_vma=False)
```

```python
import functools

import jax
import jax.numpy as jnp
from jax import lax
from jax.experimental import pallas as pl
from jax.experimental.pallas import tpu as pltpu
from jax.sharding import PartitionSpec as P

TAPS = 9
REACH = 4
ARRIVE = (7, 3, 6, 2, 5, 1, 4)
SPANS = ((0, 4), (6, 8), (4, 6))


def with_halo(block, sides, width):
    for axis, dim in sides:
        count = lax.axis_size(axis)
        forward = [(i, i + 1) for i in range(count - 1)]
        backward = [(target, source) for source, target in forward]
        low = lax.ppermute(
            lax.slice_in_dim(block, block.shape[dim] - width, None, axis=dim), axis, forward
        )
        high = lax.ppermute(lax.slice_in_dim(block, 0, width, axis=dim), axis, backward)
        block = jnp.concatenate([low, block, high], axis=dim)
    return block


def horizontal(values, root_tiles, col_index):
    slot_count, block_size = (root_tiles.shape[0], root_tiles.shape[1])
    members, levels, columns = values.shape
    row_blocks = columns // block_size
    blocks = values.reshape(members, levels, row_blocks, block_size)
    picked = jnp.take(blocks, col_index.reshape(-1), axis=2)
    picked = picked.reshape(members * levels * row_blocks, slot_count * block_size)
    stacked = root_tiles.reshape(slot_count * block_size, block_size)
    product = jnp.dot(
        picked, stacked, precision=lax.Precision.HIGHEST, preferred_element_type=jnp.float32
    )
    return product.reshape(values.shape)


def horizontal_t(values, root_tiles, col_index):
    slot_count, block_size = (root_tiles.shape[0], root_tiles.shape[1])
    members, levels, columns = values.shape
    row_blocks = columns // block_size
    flat = values.reshape(-1, block_size)
    stacked = jnp.transpose(root_tiles, (2, 0, 1)).reshape(block_size, slot_count * block_size)
    product = jnp.dot(
        flat, stacked, precision=lax.Precision.HIGHEST, preferred_element_type=jnp.float32
    )
    product = product.reshape(members, levels, row_blocks * slot_count, block_size)
    summed = jnp.zeros((members, levels, row_blocks, block_size), jnp.float32)
    summed = summed.at[:, :, col_index.reshape(-1), :].add(product)
    return summed.reshape(values.shape)


def general_body(
    ensemble, innovation, obs_inverse, root_tiles, col_index, vert_weight, member_weight, obs_blocks
):
    block_size = root_tiles.shape[1]
    lev_dev = ensemble.shape[1]
    col_dev = ensemble.shape[2]
    wide_count = lax.axis_size("wide")
    first_block = lax.axis_index("wide") * (col_dev // block_size)
    block_ids = first_block + jnp.arange(col_dev // block_size, dtype=jnp.int32)
    counts = jnp.sum((obs_blocks[:, None] == block_ids[None, :]).astype(jnp.float32), axis=0)
    obs_weight = obs_inverse * jnp.repeat(counts, block_size)[None, :]
    padded_weights = jnp.pad(vert_weight, ((0, 0), (4, 4)))
    level_start = lax.axis_index("lev") * lev_dev
    wide_weights = lax.dynamic_slice_in_dim(padded_weights, level_start, lev_dev + 8, 1)
    own_weights = wide_weights[:, 4 : 4 + lev_dev]
    weighted = member_weight[:, None, None] * ensemble

    def grouped(values):
        return values.reshape(wide_count, values.shape[0] // wide_count, lev_dev, col_dev)

    values = lax.all_to_all(
        grouped(weighted * (-(obs_weight * innovation))[None]),
        "wide",
        split_axis=0,
        concat_axis=3,
        tiled=True,
    )[0]
    blended = horizontal_t(values, root_tiles, col_index)
    padded = with_halo(blended, (("lev", 1),), 4)
    summed = jnp.zeros(values.shape, jnp.float32)
    for reverse_offset in range(9):
        lower = 8 - reverse_offset
        summed = (
            summed
            + wide_weights[reverse_offset, lower : lower + lev_dev][None, :, None]
            * padded[:, lower : lower + lev_dev]
        )
    member_fields = summed[None]
    gradient = lax.all_to_all(member_fields[0], "wide", split_axis=2, concat_axis=0, tiled=True)
    control = jnp.zeros_like(gradient)
    increment = jnp.zeros_like(innovation)
    values = lax.all_to_all(grouped(gradient), "wide", split_axis=0, concat_axis=3, tiled=True)[0]
    padded = with_halo(values, (("lev", 1),), 4)
    blended = jnp.zeros(values.shape, jnp.float32)
    for offset in range(9):
        blended = (
            blended + own_weights[offset][None, :, None] * padded[:, offset : offset + lev_dev]
        )
    mapped = horizontal(blended, root_tiles, col_index)[None]
    by_column = lax.all_to_all(mapped[0], "wide", split_axis=2, concat_axis=0, tiled=True)
    image_field = jnp.sum(weighted * by_column, axis=0)
    grad_norm, observed = lax.psum(
        (jnp.sum(gradient * gradient), jnp.sum(obs_weight * image_field * image_field)),
        ("wide", "lev"),
    )
    curvature = grad_norm + observed
    step_size = grad_norm / curvature
    control = control - step_size * gradient
    increment = increment - step_size * image_field
    return (control, increment)


CHAIN = (4, 2, 1)
UNROLL_PAIRS = 8
UNROLL_MEMBERS = 16
UNROLL_SUM = 16
SPREAD_ROOM = 8
PREPARE_ROOM = 16
MEMBER_ROOM = 24
FINISH_ROOM = 8


def split_high_low(values):
    high = values.astype(jnp.bfloat16)
    return high, (values - high.astype(jnp.float32)).astype(jnp.bfloat16)


SCALARS = pl.BlockSpec(memory_space=pltpu.SMEM)
IN_PLACE = pl.BlockSpec(memory_space=pltpu.HBM)
ON_CHIP = pl.BlockSpec(memory_space=pltpu.VMEM)


def in_place(operand):
    return pltpu.with_memory_space_constraint(operand, pltpu.HBM)


def room(mebibytes):
    return pltpu.CompilerParams(vmem_limit_bytes=mebibytes << 20)


def spread_kernel(ens_any, inverse_any, innov_any, seen_any, *refs):
    wide = ens_any.shape[0]
    blocks, (inverse, innov, seen, sems) = refs[:wide], refs[wide:]
    members = ens_any.shape[1]
    place = lax.axis_index("wide")
    small = [
        pltpu.make_async_copy(seen_any, seen, sems.at[wide]),
        pltpu.make_async_copy(inverse_any, inverse, sems.at[wide + 1]),
        pltpu.make_async_copy(innov_any, innov, sems.at[wide + 2]),
    ]
    fetches = [
        pltpu.make_async_copy(
            ens_any.at[place ^ other], blocks[other].at[pl.ds(0, members)], sems.at[other]
        )
        for other in (*ARRIVE, 0)
        if other < wide
    ]
    for fetch in small + fetches:
        fetch.start()
    for fetch in small:
        fetch.wait()
    count = lax.fori_loop(
        0,
        seen.shape[0],
        lambda i, total: total + (seen[i] == place).astype(jnp.int32),
        jnp.int32(0),
    )
    weight = inverse[...] * count.astype(jnp.float32)
    source = -(weight * innov[...])
    for block in blocks:
        block[members] = source
        block[members + 1] = weight
    for fetch in fetches:
        fetch.wait()


def spread(ensemble, obs_inverse, innovation, obs_blocks):
    wide, members, lev_dev, size = ensemble.shape
    block = jax.ShapeDtypeStruct((members + 2, lev_dev, size), jnp.float32)
    return pl.pallas_call(
        spread_kernel,
        out_shape=[block] * wide,
        in_specs=[IN_PLACE] * 4,
        out_specs=[ON_CHIP] * wide,
        scratch_shapes=[
            pltpu.VMEM((lev_dev, size), jnp.float32),
            pltpu.VMEM((lev_dev, size), jnp.float32),
            pltpu.SMEM(obs_blocks.shape, jnp.int32),
            pltpu.SemaphoreType.DMA((wide + 3,)),
        ],
        compiler_params=room(SPREAD_ROOM),
        cost_estimate=pl.CostEstimate(
            flops=0, bytes_accessed=8 * ensemble.size, transcendentals=0
        ),
    )(*map(in_place, (ensemble, obs_inverse, innovation, obs_blocks)))


def prepare_kernel(
    col_any, tiles_any, weight_ref, high_ref, low_ref, taps_ref, root, col_ref, tiles_ref, sems
):
    blocks, slots = col_ref.shape
    size = tiles_ref.shape[1]
    fetches = [
        pltpu.make_async_copy(col_any, col_ref, sems.at[0]),
        pltpu.make_async_copy(tiles_any, tiles_ref, sems.at[1]),
    ]
    for fetch in fetches:
        fetch.start()
    lev_dev = taps_ref.shape[1] - 2 * REACH
    place, level_start = lax.axis_index("wide"), lax.axis_index("lev") * lev_dev
    root[...] = jnp.zeros_like(root)
    for fetch in fetches:
        fetch.wait()

    @pl.loop(0, slots)
    def _(slot):
        tile = tiles_ref[slot]
        for row in range(blocks):
            lanes = pl.ds(pl.multiple_of((row ^ place) * size, size), size)
            root[col_ref[row, slot] ^ place, :, lanes] += tile

    @pl.loop(0, blocks)
    def _(block):
        high, low = split_high_low(root[block])
        start = pl.multiple_of(block * size, size)
        high_ref[pl.ds(start, size), :] = high
        low_ref[pl.ds(start, size), :] = low

    outer = taps_ref.shape[1]
    levels = weight_ref.shape[0] - 4 * REACH
    window = weight_ref[pl.ds(pl.multiple_of(level_start, 8), lev_dev + 4 * REACH), :]
    target = level_start - REACH + lax.broadcasted_iota(jnp.int32, (outer, size), 0)
    inside = (target >= 0) & (target < levels)
    own = window[2 * REACH :]
    for tap in range(TAPS):
        column = pltpu.roll(window, (-tap) % window.shape[0], 0)[:outer] if tap else window[:outer]
        column = column[:, TAPS - 1 - tap : TAPS - tap]
        taps_ref[tap] = jnp.where(inside, jnp.broadcast_to(column, (outer, size)), 0.0)
        taps_ref[TAPS + tap] = jnp.broadcast_to(own[:outer, tap : tap + 1], (outer, size))


def prepare(root_tiles, col_index, vert_weight, lev_dev):
    size = root_tiles.shape[1]
    blocks = col_index.shape[0]
    columns = blocks * size
    outer = lev_dev + 2 * REACH
    weights = jnp.pad(vert_weight.T, ((2 * REACH, 2 * REACH), (0, 128 - TAPS)))
    part = jax.ShapeDtypeStruct((columns, columns), jnp.bfloat16)
    taps = jax.ShapeDtypeStruct((2 * TAPS, outer, size), jnp.float32)
    return pl.pallas_call(
        prepare_kernel,
        out_shape=(part, part, taps),
        in_specs=[IN_PLACE, IN_PLACE, ON_CHIP],
        out_specs=[ON_CHIP] * 3,
        scratch_shapes=[
            pltpu.VMEM((blocks, size, columns), jnp.float32),
            pltpu.SMEM(col_index.shape, jnp.int32),
            pltpu.VMEM(root_tiles.shape, jnp.float32),
            pltpu.SemaphoreType.DMA((2,)),
        ],
        compiler_params=room(PREPARE_ROOM),
        cost_estimate=pl.CostEstimate(
            flops=8 * columns * columns, bytes_accessed=8 * columns * columns, transcendentals=0
        ),
    )(in_place(col_index), in_place(root_tiles), weights)


def vertical(values, taps, first, count):
    rows = values.shape[0]
    total = taps[first, :count] * values[:count]
    for tap in range(1, TAPS):
        total = total + taps[first + tap, :count] * pltpu.roll(values, rows - tap, 0)[:count]
    return total


def three_pass(parts, rows, high, low, contract):
    dims = (((1,), (contract,)), ((), ()))
    both = lax.dot_general(parts[...], high, dims, preferred_element_type=jnp.float32)
    small = lax.dot_general(parts[:rows, :], low, dims, preferred_element_type=jnp.float32)
    return both[:rows] + (both[rows:] + small)


def gradient_kernel(begin, first, weight_ref, taps_ref, high, low, far, near, *refs):
    count = far.shape[0]
    ens, refs = refs[:count], refs[count:]
    if not first:
        sofar, refs = refs[0], refs[1:]
    field, parts, grads = refs[0], refs[-1], refs[1:-1]
    slots, lev_dev, size = ens[0].shape
    members = slots - 2
    columns = high.shape[0]
    outer = lev_dev + 2 * REACH
    rows = members * outer
    first_weight = lax.axis_index("wide") * members
    odd = lax.axis_index("lev") % 2 == 1
    for block in range(count):

        def extended(member):
            one, two = far[block, member], near[block, member]
            below, above = jnp.where(odd, two, one), jnp.where(odd, one, two)
            return jnp.concatenate([below, ens[block][member], above], axis=0)

        source = extended(members)
        lanes = slice(block * size, (block + 1) * size)

        @pl.loop(0, members // 2, unroll=UNROLL_PAIRS)
        def _(pair):
            pieces = []
            for half in range(2):
                member = 2 * pair + half
                product = weight_ref[first_weight + member] * (extended(member) * source)
                pieces.append(vertical(product, taps_ref, 0, outer))
            upper, lower = split_high_low(jnp.concatenate(pieces, axis=0))
            start = pl.multiple_of(pair * 2 * outer, 2 * outer)
            parts[pl.ds(start, 2 * outer), lanes] = upper
            start = pl.multiple_of(rows + pair * 2 * outer, 2 * outer)
            parts[pl.ds(start, 2 * outer), lanes] = lower

    span = slice(begin * size, (begin + count) * size)
    step = min(2 * size, columns)
    for at in range(0, columns, step):
        total = three_pass(parts, rows, high[at : at + step, span], low[at : at + step, span], 1)
        if not first:
            total = total + sofar[:, at : at + step]
        field[:, at : at + step] = total
    for block, grad in enumerate(grads):
        lanes = slice(block * size, (block + 1) * size)
        for member in range(members):
            start = member * outer + REACH
            grad[member] = field[start : start + lev_dev, lanes]


def gradient_part(weights, taps, high, low, halo_pair, arrived, begin, sofar, last):
    slots, lev_dev, size = arrived[0].shape
    members = slots - 2
    columns = high.shape[0]
    rows = members * (lev_dev + 2 * REACH)
    field = jax.ShapeDtypeStruct((rows, columns), jnp.float32)
    grads = [jax.ShapeDtypeStruct((members, lev_dev, size), jnp.float32)] * (columns // size)
    outs = [field] + (grads if last else [])
    operands = [taps, high, low, *halo_pair, *arrived] + ([] if sofar is None else [sofar])
    span = len(arrived) * size
    return pl.pallas_call(
        functools.partial(gradient_kernel, begin, sofar is None),
        out_shape=outs,
        in_specs=[SCALARS] + [ON_CHIP] * len(operands),
        out_specs=[ON_CHIP] * len(outs),
        scratch_shapes=[pltpu.VMEM((2 * rows, span), jnp.bfloat16)],
        compiler_params=room(MEMBER_ROOM),
        cost_estimate=pl.CostEstimate(
            flops=6 * rows * columns * span, bytes_accessed=4 * rows * columns, transcendentals=0
        ),
    )(weights, *operands)


def image_kernel(weight_ref, taps_ref, high, low, field, *refs):
    ens, (image_ref, parts, mapped) = refs[:-3], refs[-3:]
    place = lax.axis_index("wide")
    slots, lev_dev, size = ens[0].shape
    members = slots - 2
    columns = high.shape[0]
    outer = lev_dev + 2 * REACH
    first_weight = lax.axis_index("wide") * members
    rows = members * lev_dev
    norm = jnp.zeros((lev_dev, size), jnp.float32)
    for block in range(len(ens)):
        lanes = slice(block * size, (block + 1) * size)

        def blend(member, norm):
            values = field[pl.ds(pl.multiple_of(member * outer, 8), outer), lanes]
            own = pltpu.roll(values, outer - REACH, 0)[:lev_dev]
            upper, lower = split_high_low(vertical(values, taps_ref, TAPS, lev_dev))
            parts[pl.ds(pl.multiple_of(member * lev_dev, lev_dev), lev_dev), lanes] = upper
            start = pl.multiple_of(rows + member * lev_dev, lev_dev)
            parts[pl.ds(start, lev_dev), lanes] = lower
            return norm + own * own

        norm = lax.fori_loop(0, members, blend, norm, unroll=UNROLL_MEMBERS)
    image_ref[len(ens)] = norm

    step = min(2 * size, columns)
    for at in range(0, columns, step):
        mapped[:, at : at + step] = three_pass(
            parts, rows, high[:, at : at + step], low[:, at : at + step], 0
        )
    for block in range(len(ens)):
        lanes = slice(block * size, (block + 1) * size)

        def add(member, total):
            start = pl.multiple_of(member * lev_dev, lev_dev)
            weighted = weight_ref[first_weight + member] * ens[block][member]
            return total + weighted * mapped[pl.ds(start, lev_dev), lanes]

        image_ref[place ^ block] = lax.fori_loop(
            0, members, add, jnp.zeros((lev_dev, size), jnp.float32), unroll=UNROLL_SUM
        )


def image_part(weights, taps, high, low, field, arrived):
    slots, lev_dev, size = arrived[0].shape
    columns = high.shape[0]
    rows = (slots - 2) * lev_dev
    return pl.pallas_call(
        image_kernel,
        out_shape=jax.ShapeDtypeStruct((len(arrived) + 1, lev_dev, size), jnp.float32),
        in_specs=[SCALARS] + [ON_CHIP] * (4 + len(arrived)),
        out_specs=ON_CHIP,
        scratch_shapes=[
            pltpu.VMEM((2 * rows, columns), jnp.bfloat16),
            pltpu.VMEM((rows, columns), jnp.float32),
        ],
        compiler_params=room(MEMBER_ROOM),
        cost_estimate=pl.CostEstimate(
            flops=6 * rows * columns * columns, bytes_accessed=4 * rows * columns, transcendentals=0
        ),
    )(weights, taps, high, low, field, *arrived)


def observe_kernel(one_ref, two_ref, *refs):
    ens, (image_ref, sums_ref) = refs[:-2], refs[-2:]
    members = ens[0].shape[0] - 2
    place = lax.axis_index("wide")
    total = jnp.zeros(image_ref.shape, jnp.float32)
    for block, ens_ref in enumerate(ens):
        image = one_ref[place ^ block] + two_ref[place ^ block]
        total = total + ens_ref[members + 1] * image * image
        if block == 0:
            image_ref[...] = image
    sums_ref[0] = one_ref[len(ens)] + two_ref[len(ens)]
    sums_ref[1] = total


def observe(one, two, arrived):
    own = one.shape[1:]
    return pl.pallas_call(
        observe_kernel,
        out_shape=[
            jax.ShapeDtypeStruct(own, jnp.float32),
            jax.ShapeDtypeStruct((2, *own), jnp.float32),
        ],
        in_specs=[ON_CHIP] * (2 + len(arrived)),
        out_specs=[ON_CHIP] * 2,
        compiler_params=room(FINISH_ROOM),
    )(one, two, *arrived)


def finish_kernel(image_ref, *refs):
    wide = len(refs) - 6
    one_ref, two_ref, grad_refs, (control_any, increment_ref, scaled, sems) = (
        *refs[:2],
        refs[2 : wide + 2],
        refs[wide + 2 :],
    )
    place = lax.axis_index("wide")
    sums = one_ref[...] + two_ref[...]
    norm = jnp.sum(sums[0], keepdims=True)
    observed = jnp.sum(sums[1], keepdims=True)
    scale = -(norm / (norm + observed))
    increment_ref[...] = scale * image_ref[...]
    stores = []
    for other, grad in enumerate(grad_refs):
        scaled[other] = scale[None] * grad[...]
        stores.append(
            pltpu.make_async_copy(scaled.at[other], control_any.at[place ^ other], sems.at[other])
        )
        stores[-1].start()
    for store in stores:
        store.wait()


def finish(image, one, two, grads):
    wide = len(grads)
    control = jax.ShapeDtypeStruct((wide, *grads[0].shape), jnp.float32)
    return pl.pallas_call(
        finish_kernel,
        out_shape=(control, jax.ShapeDtypeStruct(image.shape, jnp.float32)),
        in_specs=[ON_CHIP] * (3 + wide),
        out_specs=[IN_PLACE, ON_CHIP],
        scratch_shapes=[
            pltpu.VMEM(control.shape, jnp.float32),
            pltpu.SemaphoreType.DMA((wide,)),
        ],
        compiler_params=room(FINISH_ROOM),
    )(image, one, two, *grads)


def swap(values, axes, other):
    count = lax.axis_size(axes)
    return lax.ppermute(values, axes, [(i, i ^ other) for i in range(count)])


def halos(arrived):
    reach = 2 * REACH
    count = lax.axis_size("lev")
    top = arrived[0].shape[1] - reach
    odd = lax.axis_index("lev") % 2
    received = []
    for start, offset in ((1, odd * top), (0, (1 - odd) * top)):
        pairs = [(i, i + 1) for i in range(start, count - 1, 2)]
        pairs += [(i + 1, i) for i in range(start, count - 1, 2)]
        edges = jnp.stack(
            [lax.dynamic_slice_in_dim(block[:-1], offset, reach, axis=1) for block in arrived]
        )
        received.append(lax.ppermute(edges, "lev", pairs))
    return received


def member_body(
    ensemble, innovation, obs_inverse, root_tiles, col_index, vert_weight, member_weight, obs_blocks
):
    wide = lax.axis_size("wide")
    members, lev_dev, size = ensemble.shape
    part = members // wide
    sent = spread(
        ensemble.reshape(wide, part, lev_dev, size), obs_inverse, innovation, obs_blocks
    )
    arrived = [sent[0]] + [None] * (wide - 1)
    for other in ARRIVE:
        if other < wide:
            arrived[other] = swap(sent[other], "wide", other)
    high, low, taps = prepare(root_tiles, col_index, vert_weight, lev_dev)
    results = (None,)
    for number, (begin, end) in enumerate(SPANS):
        group = arrived[begin * wide // 8 : end * wide // 8]
        halo_pair = halos(group)
        results = gradient_part(
            member_weight, taps, high, low, halo_pair, group, begin * wide // 8,
            results[0], number == len(SPANS) - 1,
        )
    field, *grads = results
    for other in range(1, wide):
        grads[other] = swap(grads[other], "wide", other)
    image = image_part(member_weight, taps, high, low, field, arrived)
    other_image = jnp.zeros_like(image)
    for step, other in enumerate(CHAIN):
        if step:
            image = image + other_image
        other_image = swap(image, "wide", other)
    image, sums = observe(image, other_image, arrived)
    step, other, other_sums = len(CHAIN), 1, jnp.zeros_like(sums)
    while other < lax.axis_size("lev"):
        if other > 1:
            sums = sums + other_sums
        other_sums = swap(sums, "lev", other)
        step, other = step + 1, other * 2
    control, increment = finish(image, sums, other_sums, grads)
    return control.reshape(ensemble.shape), increment


def solution(mesh):
    in_specs = (P(None, "lev", "wide"), P("lev", "wide"), P("lev", "wide"), P(), P(), P(), P(), P())
    out_specs = (P(None, "lev", "wide"), P("lev", "wide"))

    def body(*args):
        ensemble, root_tiles = args[0], args[3]
        wide, lev = lax.axis_size("wide"), lax.axis_size("lev")
        members, lev_dev, col_dev = ensemble.shape
        fits = (
            wide & (wide - 1) == 0
            and lev & (lev - 1) == 0
            and wide == 8
            and members % (2 * wide) == 0
            and lev_dev % 16 == 0
            and col_dev == root_tiles.shape[1] == 128
        )
        if not fits:
            return general_body(*args)
        return member_body(*args)

    return jax.shard_map(body, mesh=mesh, in_specs=in_specs, out_specs=out_specs, check_vma=False)
```

```python
import functools

import jax
import jax.numpy as jnp
from jax import lax
from jax.experimental import pallas as pl
from jax.experimental.pallas import tpu as pltpu
from jax.sharding import PartitionSpec as P

TAPS = 9
REACH = 4
ARRIVE = (7, 3, 6, 2, 5, 1, 4)
SPANS = ((0, 4), (6, 8), (4, 6))


def with_halo(block, sides, width):
    for axis, dim in sides:
        count = lax.axis_size(axis)
        forward = [(i, i + 1) for i in range(count - 1)]
        backward = [(target, source) for source, target in forward]
        low = lax.ppermute(
            lax.slice_in_dim(block, block.shape[dim] - width, None, axis=dim), axis, forward
        )
        high = lax.ppermute(lax.slice_in_dim(block, 0, width, axis=dim), axis, backward)
        block = jnp.concatenate([low, block, high], axis=dim)
    return block


def horizontal(values, root_tiles, col_index):
    slot_count, block_size = (root_tiles.shape[0], root_tiles.shape[1])
    members, levels, columns = values.shape
    row_blocks = columns // block_size
    blocks = values.reshape(members, levels, row_blocks, block_size)
    picked = jnp.take(blocks, col_index.reshape(-1), axis=2)
    picked = picked.reshape(members * levels * row_blocks, slot_count * block_size)
    stacked = root_tiles.reshape(slot_count * block_size, block_size)
    product = jnp.dot(
        picked, stacked, precision=lax.Precision.HIGHEST, preferred_element_type=jnp.float32
    )
    return product.reshape(values.shape)


def horizontal_t(values, root_tiles, col_index):
    slot_count, block_size = (root_tiles.shape[0], root_tiles.shape[1])
    members, levels, columns = values.shape
    row_blocks = columns // block_size
    flat = values.reshape(-1, block_size)
    stacked = jnp.transpose(root_tiles, (2, 0, 1)).reshape(block_size, slot_count * block_size)
    product = jnp.dot(
        flat, stacked, precision=lax.Precision.HIGHEST, preferred_element_type=jnp.float32
    )
    product = product.reshape(members, levels, row_blocks * slot_count, block_size)
    summed = jnp.zeros((members, levels, row_blocks, block_size), jnp.float32)
    summed = summed.at[:, :, col_index.reshape(-1), :].add(product)
    return summed.reshape(values.shape)


def general_body(
    ensemble, innovation, obs_inverse, root_tiles, col_index, vert_weight, member_weight, obs_blocks
):
    block_size = root_tiles.shape[1]
    lev_dev = ensemble.shape[1]
    col_dev = ensemble.shape[2]
    wide_count = lax.axis_size("wide")
    first_block = lax.axis_index("wide") * (col_dev // block_size)
    block_ids = first_block + jnp.arange(col_dev // block_size, dtype=jnp.int32)
    counts = jnp.sum((obs_blocks[:, None] == block_ids[None, :]).astype(jnp.float32), axis=0)
    obs_weight = obs_inverse * jnp.repeat(counts, block_size)[None, :]
    padded_weights = jnp.pad(vert_weight, ((0, 0), (4, 4)))
    level_start = lax.axis_index("lev") * lev_dev
    wide_weights = lax.dynamic_slice_in_dim(padded_weights, level_start, lev_dev + 8, 1)
    own_weights = wide_weights[:, 4 : 4 + lev_dev]
    weighted = member_weight[:, None, None] * ensemble

    def grouped(values):
        return values.reshape(wide_count, values.shape[0] // wide_count, lev_dev, col_dev)

    values = lax.all_to_all(
        grouped(weighted * (-(obs_weight * innovation))[None]),
        "wide",
        split_axis=0,
        concat_axis=3,
        tiled=True,
    )[0]
    blended = horizontal_t(values, root_tiles, col_index)
    padded = with_halo(blended, (("lev", 1),), 4)
    summed = jnp.zeros(values.shape, jnp.float32)
    for reverse_offset in range(9):
        lower = 8 - reverse_offset
        summed = (
            summed
            + wide_weights[reverse_offset, lower : lower + lev_dev][None, :, None]
            * padded[:, lower : lower + lev_dev]
        )
    member_fields = summed[None]
    gradient = lax.all_to_all(member_fields[0], "wide", split_axis=2, concat_axis=0, tiled=True)
    control = jnp.zeros_like(gradient)
    increment = jnp.zeros_like(innovation)
    values = lax.all_to_all(grouped(gradient), "wide", split_axis=0, concat_axis=3, tiled=True)[0]
    padded = with_halo(values, (("lev", 1),), 4)
    blended = jnp.zeros(values.shape, jnp.float32)
    for offset in range(9):
        blended = (
            blended + own_weights[offset][None, :, None] * padded[:, offset : offset + lev_dev]
        )
    mapped = horizontal(blended, root_tiles, col_index)[None]
    by_column = lax.all_to_all(mapped[0], "wide", split_axis=2, concat_axis=0, tiled=True)
    image_field = jnp.sum(weighted * by_column, axis=0)
    grad_norm, observed = lax.psum(
        (jnp.sum(gradient * gradient), jnp.sum(obs_weight * image_field * image_field)),
        ("wide", "lev"),
    )
    curvature = grad_norm + observed
    step_size = grad_norm / curvature
    control = control - step_size * gradient
    increment = increment - step_size * image_field
    return (control, increment)


CHAIN = (4, 2)
UNROLL_PAIRS = 8
UNROLL_MEMBERS = 16
UNROLL_SUM = 16
SPREAD_ROOM = 8
PREPARE_ROOM = 16
MEMBER_ROOM = 24
FINISH_ROOM = 8


def split_high_low(values):
    high = values.astype(jnp.bfloat16)
    return high, (values - high.astype(jnp.float32)).astype(jnp.bfloat16)


SCALARS = pl.BlockSpec(memory_space=pltpu.SMEM)
IN_PLACE = pl.BlockSpec(memory_space=pltpu.HBM)
ON_CHIP = pl.BlockSpec(memory_space=pltpu.VMEM)


def in_place(operand):
    return pltpu.with_memory_space_constraint(operand, pltpu.HBM)


def room(mebibytes):
    return pltpu.CompilerParams(vmem_limit_bytes=mebibytes << 20)


def spread_kernel(ens_any, inverse_any, innov_any, seen_any, *refs):
    wide = ens_any.shape[0]
    blocks, (inverse, innov, seen, sems) = refs[:wide], refs[wide:]
    members = ens_any.shape[1]
    place = lax.axis_index("wide")
    small = [
        pltpu.make_async_copy(seen_any, seen, sems.at[wide]),
        pltpu.make_async_copy(inverse_any, inverse, sems.at[wide + 1]),
        pltpu.make_async_copy(innov_any, innov, sems.at[wide + 2]),
    ]
    fetches = [
        pltpu.make_async_copy(
            ens_any.at[place ^ other], blocks[other].at[pl.ds(0, members)], sems.at[other]
        )
        for other in (*ARRIVE, 0)
        if other < wide
    ]
    for fetch in small + fetches:
        fetch.start()
    for fetch in small:
        fetch.wait()
    count = lax.fori_loop(
        0,
        seen.shape[0],
        lambda i, total: total + (seen[i] == place).astype(jnp.int32),
        jnp.int32(0),
    )
    weight = inverse[...] * count.astype(jnp.float32)
    source = -(weight * innov[...])
    for block in blocks:
        block[members] = source
        block[members + 1] = weight
    for fetch in fetches:
        fetch.wait()


def spread(ensemble, obs_inverse, innovation, obs_blocks):
    wide, members, lev_dev, size = ensemble.shape
    block = jax.ShapeDtypeStruct((members + 2, lev_dev, size), jnp.float32)
    return pl.pallas_call(
        spread_kernel,
        out_shape=[block] * wide,
        in_specs=[IN_PLACE] * 4,
        out_specs=[ON_CHIP] * wide,
        scratch_shapes=[
            pltpu.VMEM((lev_dev, size), jnp.float32),
            pltpu.VMEM((lev_dev, size), jnp.float32),
            pltpu.SMEM(obs_blocks.shape, jnp.int32),
            pltpu.SemaphoreType.DMA((wide + 3,)),
        ],
        compiler_params=room(SPREAD_ROOM),
        cost_estimate=pl.CostEstimate(
            flops=0, bytes_accessed=8 * ensemble.size, transcendentals=0
        ),
    )(*map(in_place, (ensemble, obs_inverse, innovation, obs_blocks)))


def prepare_kernel(
    col_any, tiles_any, weight_ref, high_ref, low_ref, taps_ref, root, col_ref, tiles_ref, sems
):
    blocks, slots = col_ref.shape
    size = tiles_ref.shape[1]
    fetches = [
        pltpu.make_async_copy(col_any, col_ref, sems.at[0]),
        pltpu.make_async_copy(tiles_any, tiles_ref, sems.at[1]),
    ]
    for fetch in fetches:
        fetch.start()
    lev_dev = taps_ref.shape[1] - 2 * REACH
    place, level_start = lax.axis_index("wide"), lax.axis_index("lev") * lev_dev
    root[...] = jnp.zeros_like(root)
    for fetch in fetches:
        fetch.wait()

    @pl.loop(0, slots)
    def _(slot):
        tile = tiles_ref[slot]
        for row in range(blocks):
            lanes = pl.ds(pl.multiple_of((row ^ place) * size, size), size)
            root[col_ref[row, slot] ^ place, :, lanes] += tile

    @pl.loop(0, blocks)
    def _(block):
        high, low = split_high_low(root[block])
        start = pl.multiple_of(block * size, size)
        high_ref[pl.ds(start, size), :] = high
        low_ref[pl.ds(start, size), :] = low

    outer = taps_ref.shape[1]
    levels = weight_ref.shape[0] - 4 * REACH
    window = weight_ref[pl.ds(pl.multiple_of(level_start, 8), lev_dev + 4 * REACH), :]
    target = level_start - REACH + lax.broadcasted_iota(jnp.int32, (outer, size), 0)
    inside = (target >= 0) & (target < levels)
    own = window[2 * REACH :]
    for tap in range(TAPS):
        column = pltpu.roll(window, (-tap) % window.shape[0], 0)[:outer] if tap else window[:outer]
        column = column[:, TAPS - 1 - tap : TAPS - tap]
        taps_ref[tap] = jnp.where(inside, jnp.broadcast_to(column, (outer, size)), 0.0)
        taps_ref[TAPS + tap] = jnp.broadcast_to(own[:outer, tap : tap + 1], (outer, size))


def prepare(root_tiles, col_index, vert_weight, lev_dev):
    size = root_tiles.shape[1]
    blocks = col_index.shape[0]
    columns = blocks * size
    outer = lev_dev + 2 * REACH
    weights = jnp.pad(vert_weight.T, ((2 * REACH, 2 * REACH), (0, 128 - TAPS)))
    part = jax.ShapeDtypeStruct((columns, columns), jnp.bfloat16)
    taps = jax.ShapeDtypeStruct((2 * TAPS, outer, size), jnp.float32)
    return pl.pallas_call(
        prepare_kernel,
        out_shape=(part, part, taps),
        in_specs=[IN_PLACE, IN_PLACE, ON_CHIP],
        out_specs=[ON_CHIP] * 3,
        scratch_shapes=[
            pltpu.VMEM((blocks, size, columns), jnp.float32),
            pltpu.SMEM(col_index.shape, jnp.int32),
            pltpu.VMEM(root_tiles.shape, jnp.float32),
            pltpu.SemaphoreType.DMA((2,)),
        ],
        compiler_params=room(PREPARE_ROOM),
        cost_estimate=pl.CostEstimate(
            flops=8 * columns * columns, bytes_accessed=8 * columns * columns, transcendentals=0
        ),
    )(in_place(col_index), in_place(root_tiles), weights)


def vertical(values, taps, first, count):
    rows = values.shape[0]
    total = taps[first, :count] * values[:count]
    for tap in range(1, TAPS):
        total = total + taps[first + tap, :count] * pltpu.roll(values, rows - tap, 0)[:count]
    return total


def three_pass(parts, rows, high, low, contract):
    dims = (((1,), (contract,)), ((), ()))
    both = lax.dot_general(parts[...], high, dims, preferred_element_type=jnp.float32)
    small = lax.dot_general(parts[:rows, :], low, dims, preferred_element_type=jnp.float32)
    return both[:rows] + (both[rows:] + small)


def gradient_kernel(begin, first, weight_ref, taps_ref, high, low, far, near, *refs):
    count = far.shape[0]
    ens, refs = refs[:count], refs[count:]
    if not first:
        sofar, refs = refs[0], refs[1:]
    field, parts, grads = refs[0], refs[-1], refs[1:-1]
    slots, lev_dev, size = ens[0].shape
    members = slots - 2
    columns = high.shape[0]
    outer = lev_dev + 2 * REACH
    rows = members * outer
    first_weight = lax.axis_index("wide") * members
    odd = lax.axis_index("lev") % 2 == 1
    for block in range(count):

        def extended(member):
            one, two = far[block, member], near[block, member]
            below, above = jnp.where(odd, two, one), jnp.where(odd, one, two)
            return jnp.concatenate([below, ens[block][member], above], axis=0)

        source = extended(members)
        lanes = slice(block * size, (block + 1) * size)

        @pl.loop(0, members // 2, unroll=UNROLL_PAIRS)
        def _(pair):
            pieces = []
            for half in range(2):
                member = 2 * pair + half
                product = weight_ref[first_weight + member] * (extended(member) * source)
                pieces.append(vertical(product, taps_ref, 0, outer))
            upper, lower = split_high_low(jnp.concatenate(pieces, axis=0))
            start = pl.multiple_of(pair * 2 * outer, 2 * outer)
            parts[pl.ds(start, 2 * outer), lanes] = upper
            start = pl.multiple_of(rows + pair * 2 * outer, 2 * outer)
            parts[pl.ds(start, 2 * outer), lanes] = lower

    span = slice(begin * size, (begin + count) * size)
    step = min(2 * size, columns)
    for at in range(0, columns, step):
        total = three_pass(parts, rows, high[at : at + step, span], low[at : at + step, span], 1)
        if not first:
            total = total + sofar[:, at : at + step]
        field[:, at : at + step] = total
    for block, grad in enumerate(grads):
        lanes = slice(block * size, (block + 1) * size)
        for member in range(members):
            start = member * outer + REACH
            grad[member] = field[start : start + lev_dev, lanes]


def gradient_part(weights, taps, high, low, halo_pair, arrived, begin, sofar, last):
    slots, lev_dev, size = arrived[0].shape
    members = slots - 2
    columns = high.shape[0]
    rows = members * (lev_dev + 2 * REACH)
    field = jax.ShapeDtypeStruct((rows, columns), jnp.float32)
    grads = [jax.ShapeDtypeStruct((members, lev_dev, size), jnp.float32)] * (columns // size)
    outs = [field] + (grads if last else [])
    operands = [taps, high, low, *halo_pair, *arrived] + ([] if sofar is None else [sofar])
    span = len(arrived) * size
    return pl.pallas_call(
        functools.partial(gradient_kernel, begin, sofar is None),
        out_shape=outs,
        in_specs=[SCALARS] + [ON_CHIP] * len(operands),
        out_specs=[ON_CHIP] * len(outs),
        scratch_shapes=[pltpu.VMEM((2 * rows, span), jnp.bfloat16)],
        compiler_params=room(MEMBER_ROOM),
        cost_estimate=pl.CostEstimate(
            flops=6 * rows * columns * span, bytes_accessed=4 * rows * columns, transcendentals=0
        ),
    )(weights, *operands)


def image_kernel(weight_ref, taps_ref, high, low, field, *refs):
    ens, (image_ref, parts, mapped) = refs[:-3], refs[-3:]
    place = lax.axis_index("wide")
    slots, lev_dev, size = ens[0].shape
    members = slots - 2
    columns = high.shape[0]
    outer = lev_dev + 2 * REACH
    first_weight = lax.axis_index("wide") * members
    rows = members * lev_dev
    norm = jnp.zeros((lev_dev, size), jnp.float32)
    for block in range(len(ens)):
        lanes = slice(block * size, (block + 1) * size)

        def blend(member, norm):
            values = field[pl.ds(pl.multiple_of(member * outer, 8), outer), lanes]
            own = pltpu.roll(values, outer - REACH, 0)[:lev_dev]
            upper, lower = split_high_low(vertical(values, taps_ref, TAPS, lev_dev))
            parts[pl.ds(pl.multiple_of(member * lev_dev, lev_dev), lev_dev), lanes] = upper
            start = pl.multiple_of(rows + member * lev_dev, lev_dev)
            parts[pl.ds(start, lev_dev), lanes] = lower
            return norm + own * own

        norm = lax.fori_loop(0, members, blend, norm, unroll=UNROLL_MEMBERS)
    image_ref[len(ens)] = norm

    step = min(2 * size, columns)
    for at in range(0, columns, step):
        mapped[:, at : at + step] = three_pass(
            parts, rows, high[:, at : at + step], low[:, at : at + step], 0
        )
    for block in range(len(ens)):
        lanes = slice(block * size, (block + 1) * size)

        def add(member, total):
            start = pl.multiple_of(member * lev_dev, lev_dev)
            weighted = weight_ref[first_weight + member] * ens[block][member]
            return total + weighted * mapped[pl.ds(start, lev_dev), lanes]

        half = len(ens) // 2
        image_ref[(1 - block % 2) * half + (place ^ block) // 2] = lax.fori_loop(
            0, members, add, jnp.zeros((lev_dev, size), jnp.float32), unroll=UNROLL_SUM
        )


def image_part(weights, taps, high, low, field, arrived):
    slots, lev_dev, size = arrived[0].shape
    columns = high.shape[0]
    rows = (slots - 2) * lev_dev
    return pl.pallas_call(
        image_kernel,
        out_shape=jax.ShapeDtypeStruct((len(arrived) + 1, lev_dev, size), jnp.float32),
        in_specs=[SCALARS] + [ON_CHIP] * (4 + len(arrived)),
        out_specs=ON_CHIP,
        scratch_shapes=[
            pltpu.VMEM((2 * rows, columns), jnp.bfloat16),
            pltpu.VMEM((rows, columns), jnp.float32),
        ],
        compiler_params=room(MEMBER_ROOM),
        cost_estimate=pl.CostEstimate(
            flops=6 * rows * columns * columns, bytes_accessed=4 * rows * columns, transcendentals=0
        ),
    )(weights, taps, high, low, field, *arrived)


def observe_kernel(one_ref, two_ref, *refs):
    ens, (image_ref, sums_ref) = refs[:-2], refs[-2:]
    members = ens[0].shape[0] - 2
    place = lax.axis_index("wide")
    total = jnp.zeros(image_ref.shape, jnp.float32)
    for at, ens_ref in enumerate(ens):
        block = (place ^ (2 * at)) // 2
        image = one_ref[block] + two_ref[block]
        total = total + ens_ref[members + 1] * image * image
        if at == 0:
            image_ref[...] = image
    sums_ref[0] = one_ref[len(ens)] + two_ref[len(ens)]
    sums_ref[1] = total


def observe(one, two, arrived):
    own = one.shape[1:]
    return pl.pallas_call(
        observe_kernel,
        out_shape=[
            jax.ShapeDtypeStruct(own, jnp.float32),
            jax.ShapeDtypeStruct((2, *own), jnp.float32),
        ],
        in_specs=[ON_CHIP] * (2 + len(arrived)),
        out_specs=[ON_CHIP] * 2,
        compiler_params=room(FINISH_ROOM),
    )(one, two, *arrived)


def finish_kernel(image_ref, *refs):
    wide = len(refs) - 6
    one_ref, two_ref, grad_refs, (control_any, increment_ref, scaled, sems) = (
        *refs[:2],
        refs[2 : wide + 2],
        refs[wide + 2 :],
    )
    place = lax.axis_index("wide")
    sums = one_ref[...] + two_ref[...]
    norm = jnp.sum(sums[0], keepdims=True)
    observed = jnp.sum(sums[1], keepdims=True)
    scale = -(norm / (norm + observed))
    increment_ref[...] = scale * image_ref[...]
    stores = []
    for other, grad in enumerate(grad_refs):
        scaled[other] = scale[None] * grad[...]
        stores.append(
            pltpu.make_async_copy(scaled.at[other], control_any.at[place ^ other], sems.at[other])
        )
        stores[-1].start()
    for store in stores:
        store.wait()


def finish(image, one, two, grads):
    wide = len(grads)
    control = jax.ShapeDtypeStruct((wide, *grads[0].shape), jnp.float32)
    return pl.pallas_call(
        finish_kernel,
        out_shape=(control, jax.ShapeDtypeStruct(image.shape, jnp.float32)),
        in_specs=[ON_CHIP] * (3 + wide),
        out_specs=[IN_PLACE, ON_CHIP],
        scratch_shapes=[
            pltpu.VMEM(control.shape, jnp.float32),
            pltpu.SemaphoreType.DMA((wide,)),
        ],
        compiler_params=room(FINISH_ROOM),
    )(image, one, two, *grads)


def swap(values, axes, other):
    count = lax.axis_size(axes)
    return lax.ppermute(values, axes, [(i, i ^ other) for i in range(count)])


def halos(arrived):
    reach = 2 * REACH
    count = lax.axis_size("lev")
    top = arrived[0].shape[1] - reach
    odd = lax.axis_index("lev") % 2
    received = []
    for start, offset in ((1, odd * top), (0, (1 - odd) * top)):
        pairs = [(i, i + 1) for i in range(start, count - 1, 2)]
        pairs += [(i + 1, i) for i in range(start, count - 1, 2)]
        edges = jnp.stack(
            [lax.dynamic_slice_in_dim(block[:-1], offset, reach, axis=1) for block in arrived]
        )
        received.append(lax.ppermute(edges, "lev", pairs))
    return received


def member_body(
    ensemble, innovation, obs_inverse, root_tiles, col_index, vert_weight, member_weight, obs_blocks
):
    wide = lax.axis_size("wide")
    members, lev_dev, size = ensemble.shape
    part = members // wide
    sent = spread(
        ensemble.reshape(wide, part, lev_dev, size), obs_inverse, innovation, obs_blocks
    )
    arrived = [sent[0]] + [None] * (wide - 1)
    for other in ARRIVE:
        if other < wide:
            arrived[other] = swap(sent[other], "wide", other)
    high, low, taps = prepare(root_tiles, col_index, vert_weight, lev_dev)
    results = (None,)
    for number, (begin, end) in enumerate(SPANS):
        group = arrived[begin * wide // 8 : end * wide // 8]
        halo_pair = halos(group)
        results = gradient_part(
            member_weight, taps, high, low, halo_pair, group, begin * wide // 8,
            results[0], number == len(SPANS) - 1,
        )
    field, *grads = results
    for other in range(1, wide):
        grads[other] = swap(grads[other], "wide", other)
    image = image_part(member_weight, taps, high, low, field, arrived)
    half = wide // 2
    kept = image[half:wide] + swap(image[:half], "wide", 1)
    image = jnp.concatenate([kept, image[wide:]], axis=0)
    other_image = jnp.zeros_like(image)
    for step, other in enumerate(CHAIN):
        if step:
            image = image + other_image
        other_image = swap(image, "wide", other)
    image, sums = observe(image, other_image, arrived[::2])
    steps = [("wide", 1)]
    while 1 << (len(steps) - 1) < lax.axis_size("lev"):
        steps.append(("lev", 1 << (len(steps) - 1)))
    steps = [steps[0], *steps[:0:-1]]
    other_sums = jnp.zeros_like(sums)
    for step, (axis, other) in enumerate(steps):
        if step:
            sums = sums + other_sums
        other_sums = swap(sums, axis, other)
    control, increment = finish(image, sums, other_sums, grads)
    return control.reshape(ensemble.shape), increment


def solution(mesh):
    in_specs = (P(None, "lev", "wide"), P("lev", "wide"), P("lev", "wide"), P(), P(), P(), P(), P())
    out_specs = (P(None, "lev", "wide"), P("lev", "wide"))

    def body(*args):
        ensemble, root_tiles = args[0], args[3]
        wide, lev = lax.axis_size("wide"), lax.axis_size("lev")
        members, lev_dev, col_dev = ensemble.shape
        fits = (
            wide & (wide - 1) == 0
            and lev & (lev - 1) == 0
            and wide == 8
            and members % (2 * wide) == 0
            and lev_dev % 16 == 0
            and col_dev == root_tiles.shape[1] == 128
        )
        if not fits:
            return general_body(*args)
        return member_body(*args)

    return jax.shard_map(body, mesh=mesh, in_specs=in_specs, out_specs=out_specs, check_vma=False)
```
